32 devices in a mesh: dp: 16 (over z, x, core), tp: 2 (over y).
Axes of the slice: x: 2, y: 2, z: 4, core: 2. Of those that a mesh axis runs over, the one named last changes fastest.
Arguments:
- tokens: bfloat16 [16, 1568, 384], P('dp', 'tp'), may hold values from -6 to 6
- cotangent: float32 [16, 1568, 384], P('dp', 'tp'), may hold values from -6 to 6
- query_weight: float32 [384, 384], P('dp', 'tp'), may hold values from -0.3125 to 0.3125
- key_weight: float32 [384, 384], P('dp', 'tp'), may hold values from -0.3125 to 0.3125
- value_weight: float32 [384, 384], P('dp', 'tp'), may hold values from -0.3125 to 0.3125
- output_weight: float32 [384, 384], P('tp', 'dp'), may hold values from -0.625 to 0.625
- up_weight: float32 [384, 1536], P('dp', 'tp'), may hold values from -0.3125 to 0.3125
- down_weight: float32 [1536, 384], P('tp', 'dp'), may hold values from -0.15625 to 0.15625
- query_momentum: float32 [384, 384], P('dp', 'tp')
- key_momentum: float32 [384, 384], P('dp', 'tp')
- value_momentum: float32 [384, 384], P('dp', 'tp')
- output_momentum: float32 [384, 384], P('tp', 'dp')
- up_momentum: float32 [384, 1536], P('dp', 'tp')
- down_momentum: float32 [1536, 384], P('tp', 'dp')
- norm_gains: float32 [2, 384], replicated, may hold values from 0.5 to 1.5
- block_biases: float32 [4, 384], replicated, may hold values from -4 to 4
- mixer_biases: float32 [2, 384], P(None, 'tp'), may hold values from -6 to 6
- hidden_bias: float32 [1536], P('tp'), may hold values from -6 to 6
- gains_first: float32 [2, 384], replicated
- gains_second: float32 [2, 384], replicated, as said below
- biases_first: float32 [4, 384], replicated
- biases_second: float32 [4, 384], replicated, as said below
- mixer_first: float32 [2, 384], P(None, 'tp')
- mixer_second: float32 [2, 384], P(None, 'tp'), as said below
- hidden_first: float32 [1536], P('tp')
- hidden_second: float32 [1536], P('tp'), as said below
Outputs:
- block_out: float32 [16, 1568, 384], P('dp', 'tp')
- input_grad: float32 [16, 1568, 384], P('dp', 'tp')
- query_grad: float32 [384, 384], P('dp', 'tp')
- key_grad: float32 [384, 384], P('dp', 'tp')
- value_grad: float32 [384, 384], P('dp', 'tp')
- output_grad: float32 [384, 384], P('tp', 'dp')
- up_grad: float32 [384, 1536], P('dp', 'tp')
- down_grad: float32 [1536, 384], P('tp', 'dp')
- query_velocity: float32 [384, 384], P('dp', 'tp')
- key_velocity: float32 [384, 384], P('dp', 'tp')
- value_velocity: float32 [384, 384], P('dp', 'tp')
- output_velocity: float32 [384, 384], P('tp', 'dp')
- up_velocity: float32 [384, 1536], P('dp', 'tp')
- down_velocity: float32 [1536, 384], P('tp', 'dp')
- query_master: float32 [384, 384], P('dp', 'tp')
- key_master: float32 [384, 384], P('dp', 'tp')
- value_master: float32 [384, 384], P('dp', 'tp')
- output_master: float32 [384, 384], P('tp', 'dp')
- up_master: float32 [384, 1536], P('dp', 'tp')
- down_master: float32 [1536, 384], P('tp', 'dp')
- query_copy: bfloat16 [384, 384], P('dp', 'tp')
- key_copy: bfloat16 [384, 384], P('dp', 'tp')
- value_copy: bfloat16 [384, 384], P('dp', 'tp')
- output_copy: bfloat16 [384, 384], P('tp', 'dp')
- up_copy: bfloat16 [384, 1536], P('dp', 'tp')
- down_copy: bfloat16 [1536, 384], P('tp', 'dp')
- gains_grad: float32 [2, 384], replicated
- biases_grad: float32 [4, 384], replicated
- mixer_grad: float32 [2, 384], P(None, 'tp')
- hidden_grad: float32 [1536], P('tp')
- gains_next: float32 [2, 384], replicated
- biases_next: float32 [4, 384], replicated
- mixer_next: float32 [2, 384], P(None, 'tp')
- hidden_next: float32 [1536], P('tp')
- gains_moment: float32 [2, 384], replicated
- biases_moment: float32 [4, 384], replicated
- mixer_moment: float32 [2, 384], P(None, 'tp')
- hidden_moment: float32 [1536], P('tp')
- gains_square: float32 [2, 384], replicated
- biases_square: float32 [4, 384], replicated
- mixer_square: float32 [2, 384], P(None, 'tp')
- hidden_square: float32 [1536], P('tp')
The draws below stay inside these ranges and needn't reach their ends.
Inputs may be any that keep to these rules, and one draw needn't show every extreme that they name: `gains_second`: positive. `biases_second`: positive. `mixer_second`: positive. `hidden_second`: positive.
All inputs are finite; a program needn't handle non-finite values.
Results may differ from the reference program's by a relative error of at most 0.014.
Values may be sent and summed in bfloat16 or wider, within the bound.
No kernel may reach another device: no remote copies, remote signals or barrier semaphores. Data moves between devices by JAX's collectives and lax.ppermute only.
A program may use at most 192 MiB of HBM per device.

```python
import math
import jax
import jax.numpy as jnp
from jax import lax

D = 384
HEADS = 6
HEAD = 64
FF = 1536
LEN = 1568
CLIPS = 1
NS_STEPS = 5
STEP = 10
SEQS = 16


def scaled_normal(key, salt, array_shape, spread_scale):
    return jax.random.normal(jax.random.fold_in(key, salt), array_shape, jnp.float32) * spread_scale


def matrix_scale():
    return 0.3 * math.sqrt(SEQS * LEN)


def vector_scale():
    return 0.05 * math.sqrt(SEQS * LEN)


def positive_draw(key, salt, array_shape):
    row_count = SEQS * LEN
    lower_log = math.log(0.0001 * row_count)
    upper_log = math.log(0.0006 * row_count)
    return jnp.exp(jax.random.uniform(jax.random.fold_in(key, salt), array_shape, jnp.float32, lower_log, upper_log))


def draw_query_momentum(key, part):
    return scaled_normal(key, 101, (D, D), matrix_scale())


def draw_key_momentum(key, part):
    return scaled_normal(key, 102, (D, D), matrix_scale())


def draw_value_momentum(key, part):
    return scaled_normal(key, 103, (D, D), matrix_scale())


def draw_output_momentum(key, part):
    return scaled_normal(key, 104, (D, D), matrix_scale())


def draw_up_momentum(key, part):
    return scaled_normal(key, 105, (D, FF), matrix_scale())


def draw_down_momentum(key, part):
    return scaled_normal(key, 106, (FF, D), matrix_scale())


def draw_gains_first(key, part):
    return scaled_normal(key, 201, (2, D), vector_scale())


def draw_gains_second(key, part):
    return positive_draw(key, 202, (2, D))


def draw_biases_first(key, part):
    return scaled_normal(key, 203, (4, D), vector_scale())


def draw_biases_second(key, part):
    return positive_draw(key, 204, (4, D))


def draw_mixer_first(key, part):
    return scaled_normal(key, 205, (2, D), vector_scale())


def draw_mixer_second(key, part):
    return positive_draw(key, 206, (2, D))


def draw_hidden_first(key, part):
    return scaled_normal(key, 207, (FF,), vector_scale())


def draw_hidden_second(key, part):
    return positive_draw(key, 208, (FF,))


def strengthened(values, stream_key, source, target, blocks, factor):
    owner, partner = [(jnp.arange(values.shape[dim]) // (values.shape[dim] // blocks)).reshape([-1 if axis == dim else 1 for axis in range(values.ndim)]) for dim in (source, target)]
    chosen = jax.random.permutation(stream_key, blocks)[partner]
    strong = (owner == chosen) | (owner == (partner + blocks // 2) % blocks)
    return jnp.where(strong, factor * values, values)


def level_of(rng, extent, pieces, least, high):
    gain = 1.0
    for dim, blocks in pieces:
        steps = jax.random.uniform(jax.random.fold_in(jax.random.fold_in(rng, 6), dim), (blocks,), jnp.float32, least / len(pieces), high / len(pieces))
        gain = gain * jnp.repeat(jnp.exp(steps), extent[dim] // blocks).reshape((-1,) + (1,) * (len(extent) - 1 - dim))
    return gain


def scatter_about(key, dims, scale, most, shards=(), held_as=jnp.bfloat16):
    level = level_of(key, dims, shards, -0.22, 0.18) if shards else 1.0
    entries = jax.random.normal(key, dims, jnp.float32) * scale * level
    return jnp.minimum(jnp.maximum(entries, -most), most).astype(held_as)


def heavy_noise(own_key, extent, deviation, reach, split, heavy, kind=jnp.bfloat16):
    array = deviation * jax.random.normal(own_key, extent, jnp.float32)
    if split:
        array = array * level_of(own_key, extent, split, -0.22, 0.18)
    return jnp.clip(strengthened(array, jax.random.fold_in(own_key, 3), *heavy), -reach, reach).astype(kind)


def setup_inputs(seed: int = 0) -> dict:
    splits = jax.random.split(jax.random.key(seed), 27)
    tokens = scatter_about(splits[0], (SEQS, LEN, D), 1.0, 6.0, ((0, 16), (1, 2)))
    cotangent = heavy_noise(splits[1], (SEQS, LEN, D), 1.0, 6.0, ((0, 16), (1, 2)), (0, 2, 16, 2.0), jnp.float32)
    query_weight = scatter_about(splits[2], (D, D), D ** -0.5, 0.3125, ((0, 16), (1, 2)), jnp.float32)
    key_weight = scatter_about(splits[3], (D, D), D ** -0.5, 0.3125, ((0, 16), (1, 2)), jnp.float32)
    value_weight = scatter_about(splits[4], (D, D), D ** -0.5, 0.3125, ((0, 16), (1, 2)), jnp.float32)
    output_weight = scatter_about(splits[5], (D, D), (D // 4) ** -0.5, 0.625, ((0, 2), (1, 16)), jnp.float32)
    up_weight = scatter_about(splits[6], (D, FF), D ** -0.5, 0.3125, ((0, 16), (1, 2)), jnp.float32)
    down_weight = scatter_about(splits[7], (FF, D), FF ** -0.5, 0.15625, ((0, 2), (1, 16)), jnp.float32)
    query_momentum = draw_query_momentum(jax.random.fold_in(splits[26], 71), 0)
    key_momentum = draw_key_momentum(jax.random.fold_in(splits[26], 71), 0)
    value_momentum = draw_value_momentum(jax.random.fold_in(splits[26], 71), 0)
    output_momentum = draw_output_momentum(jax.random.fold_in(splits[26], 71), 0)
    up_momentum = draw_up_momentum(jax.random.fold_in(splits[26], 71), 0)
    down_momentum = draw_down_momentum(jax.random.fold_in(splits[26], 71), 0)
    norm_gains = jnp.clip(1.0 + 0.1 * jax.random.normal(splits[14], (2, D), jnp.float32), 0.5, 1.5)
    block_biases = scatter_about(splits[15], (4, D), 0.3, 4.0, (), jnp.float32)
    mixer_biases = scatter_about(splits[16], (2, D), 0.5, 6.0, ((1, 2),), jnp.float32)
    hidden_bias = scatter_about(splits[17], (FF,), 0.5, 6.0, ((0, 2),), jnp.float32)
    gains_first = draw_gains_first(jax.random.fold_in(splits[26], 71), 0)
    gains_second = draw_gains_second(jax.random.fold_in(splits[26], 71), 0)
    biases_first = draw_biases_first(jax.random.fold_in(splits[26], 71), 0)
    biases_second = draw_biases_second(jax.random.fold_in(splits[26], 71), 0)
    mixer_first = draw_mixer_first(jax.random.fold_in(splits[26], 71), 0)
    mixer_second = draw_mixer_second(jax.random.fold_in(splits[26], 71), 0)
    hidden_first = draw_hidden_first(jax.random.fold_in(splits[26], 71), 0)
    hidden_second = draw_hidden_second(jax.random.fold_in(splits[26], 71), 0)
    return {"tokens": tokens, "cotangent": cotangent, "query_weight": query_weight, "key_weight": key_weight, "value_weight": value_weight, "output_weight": output_weight, "up_weight": up_weight, "down_weight": down_weight, "query_momentum": query_momentum, "key_momentum": key_momentum, "value_momentum": value_momentum, "output_momentum": output_momentum, "up_momentum": up_momentum, "down_momentum": down_momentum, "norm_gains": norm_gains, "block_biases": block_biases, "mixer_biases": mixer_biases, "hidden_bias": hidden_bias, "gains_first": gains_first, "gains_second": gains_second, "biases_first": biases_first, "biases_second": biases_second, "mixer_first": mixer_first, "mixer_second": mixer_second, "hidden_first": hidden_first, "hidden_second": hidden_second}


@jax.custom_vjp
def low(v):
    return lax.optimization_barrier(v.astype(jnp.bfloat16)).astype(jnp.float32)

@jax.custom_vjp
def low_back(v):
    return v

def low_keep(v):
    return (low(v), None)

def low_pass(kept, grad):
    return (grad,)

def back_keep(v):
    return (v, None)

def back_low(kept, grad):
    return (low(grad),)
low.defvjp(low_keep, low_pass)
low_back.defvjp(back_keep, back_low)
precise = lax.Precision.HIGHEST
norm_eps = 1e-06
frob_eps = 1e-07
coef_first = 3.4445
coef_second = -4.775
coef_third = 2.0315
muon_rate = 0.5
adam_rate = 0.5
decay_first = 0.9
decay_second = 0.999

def layer_norm(inputs, gain_row, shift_row):
    average = lax.optimization_barrier(jnp.mean(inputs, -1, keepdims=True))
    centred = inputs - average
    spread = lax.optimization_barrier(jnp.mean(centred * centred, -1, keepdims=True))
    return centred * lax.rsqrt(spread + norm_eps) * gain_row + shift_row

def layer(params, inputs):
    query_weight, key_weight, value_weight, output_weight, up_weight, down_weight, norm_gains, block_biases, mixer_biases, hidden_bias = params
    group_size = inputs.shape[0]
    token_rows = inputs.reshape(-1, D)
    normed_one = low(layer_norm(token_rows, norm_gains[0], block_biases[0]))
    queries = low(low_back(jnp.dot(normed_one, query_weight, precision=precise) + mixer_biases[0]))
    key_rows = low(low_back(jnp.dot(normed_one, key_weight, precision=precise)))
    value_rows = low(low_back(jnp.dot(normed_one, value_weight, precision=precise) + mixer_biases[1]))
    head_shape = (group_size, LEN, HEADS, HEAD)
    scores = low_back(jnp.einsum('cqhd,ckhd->chqk', queries.reshape(head_shape), key_rows.reshape(head_shape), precision=precise)) * HEAD ** (-0.5)
    weights_all = jax.nn.softmax(scores, -1)
    mixed_rows = jnp.einsum('chqk,ckhd->cqhd', low(weights_all), value_rows.reshape(head_shape), precision=precise)
    mixed_low = low(low_back(mixed_rows.reshape(-1, D)))
    residual = token_rows + low_back(jnp.dot(mixed_low, output_weight, precision=precise)) + block_biases[1]
    normed_two = low(layer_norm(residual, norm_gains[1], block_biases[2]))
    hidden_pre = low_back(jnp.dot(normed_two, up_weight, precision=precise) + hidden_bias)
    hidden_low = low(jax.nn.gelu(hidden_pre, approximate=False))
    block_out = residual + low_back(jnp.dot(hidden_low, down_weight, precision=precise)) + block_biases[3]
    return block_out.reshape(inputs.shape)

def orthogonalize(matrix):
    current = matrix / (jnp.sqrt(jnp.sum(matrix * matrix)) + frob_eps)
    for turn_index in range(NS_STEPS):
        gram_matrix = jnp.dot(current, current.T, precision=precise)
        first_power = jnp.dot(gram_matrix, current, precision=precise)
        second_power = jnp.dot(gram_matrix, first_power, precision=precise)
        current = coef_first * current + coef_second * first_power + coef_third * second_power
    return current

def adam_step(vector, gradient, moment, square):
    moment_next = decay_first * moment + (1.0 - decay_first) * gradient
    square_next = decay_second * square + (1.0 - decay_second) * gradient * gradient
    moment_hat = moment_next / (1.0 - decay_first ** STEP)
    square_hat = square_next / (1.0 - decay_second ** STEP)
    return (vector - adam_rate * moment_hat / (jnp.sqrt(square_hat) + 1e-08), moment_next, square_next)

def reference(tokens, cotangent, query_weight, key_weight, value_weight, output_weight, up_weight, down_weight, query_momentum, key_momentum, value_momentum, output_momentum, up_momentum, down_momentum, norm_gains, block_biases, mixer_biases, hidden_bias, gains_first, gains_second, biases_first, biases_second, mixer_first, mixer_second, hidden_first, hidden_second):
    masters = (query_weight, key_weight, value_weight, output_weight, up_weight, down_weight)
    momenta = (query_momentum, key_momentum, value_momentum, output_momentum, up_momentum, down_momentum)
    params = tuple((low(master) for master in masters)) + (norm_gains, block_biases, mixer_biases, hidden_bias)
    groups = SEQS // CLIPS
    inputs = tokens.astype(jnp.float32).reshape(groups, CLIPS, LEN, D)
    cot_groups = cotangent.astype(jnp.float32).reshape(groups, CLIPS, LEN, D)

    def one_group(totals, pair_arrays):
        outputs, pullback = jax.vjp(layer, params, pair_arrays[0])
        param_grads, input_grads = pullback(pair_arrays[1])
        return (jax.tree.map(lambda left, right: left + right, totals, param_grads), (outputs, input_grads))
    zeros = tuple((jnp.zeros(param_array.shape, jnp.float32) for param_array in params))
    grads, (block_out, input_grad) = lax.scan(one_group, zeros, (inputs, cot_groups))
    velocities = tuple((0.5 * old + gradient for old, gradient in zip(momenta, grads[:6])))
    oriented = (velocities[0], velocities[1], velocities[2], velocities[3].T, velocities[4], velocities[5].T)
    orthed = [orthogonalize(matrix) for matrix in oriented]
    restored = (orthed[0], orthed[1], orthed[2], orthed[3].T, orthed[4], orthed[5].T)
    new_masters = tuple((master - muon_rate * max(1.0, master.shape[1] / master.shape[0]) ** 0.5 * direction for master, direction in zip(masters, restored)))
    copies = tuple((master.astype(jnp.bfloat16) for master in new_masters))
    gains_next, gains_moment, gains_square = adam_step(norm_gains, grads[6], gains_first, gains_second)
    biases_next, biases_moment, biases_square = adam_step(block_biases, grads[7], biases_first, biases_second)
    mixer_next, mixer_moment, mixer_square = adam_step(mixer_biases, grads[8], mixer_first, mixer_second)
    hidden_next, hidden_moment, hidden_square = adam_step(hidden_bias, grads[9], hidden_first, hidden_second)
    return (block_out.reshape(SEQS, LEN, D), input_grad.reshape(SEQS, LEN, D), grads[0], grads[1], grads[2], grads[3], grads[4], grads[5], velocities[0], velocities[1], velocities[2], velocities[3], velocities[4], velocities[5], new_masters[0], new_masters[1], new_masters[2], new_masters[3], new_masters[4], new_masters[5], copies[0], copies[1], copies[2], copies[3], copies[4], copies[5], grads[6], grads[7], grads[8], grads[9], gains_next, biases_next, mixer_next, hidden_next, gains_moment, biases_moment, mixer_moment, hidden_moment, gains_square, biases_square, mixer_square, hidden_square)
```

```python
import functools
import math

import jax
import jax.numpy as jnp
from jax import lax
from jax.experimental import pallas as pl
from jax.experimental.pallas import tpu as pltpu
from jax.sharding import PartitionSpec as P

D = 384
HEADS = 6
HEAD = 64
FF = 1536
NS_STEPS = 5
STEP = 10


norm_eps = 1e-06
frob_eps = 1e-07
coef_first = 3.4445
coef_second = -4.775
coef_third = 2.0315
muon_rate = 0.5
adam_rate = 0.5
decay_first = 0.9
decay_second = 0.999

f32 = jnp.float32
bf16 = jnp.bfloat16
NN = (((1,), (0,)), ((), ()))
NT = (((1,), (1,)), ((), ()))
TN = (((0,), (0,)), ((), ()))
PAIR = 2 * HEAD
exact = lax.Precision.HIGHEST


def dot(left, right, dims=NN):
    return lax.dot_general(left, right, dims, preferred_element_type=f32)


def bit_of(stage):
    if stage == "tp":
        return lax.axis_index("tp")
    return (lax.axis_index("dp") >> stage) & 1


def swap(value, stage):
    if stage == "tp":
        return lax.ppermute(value, "tp", [(0, 1), (1, 0)])
    mask = 1 << stage
    return lax.ppermute(value, "dp", [(j, j ^ mask) for j in range(lax.axis_size("dp"))])


def rank_of(stage):
    return 1000 if stage == "tp" else stage


def gather_blocks(value, order, present=()):
    held = sorted(present, key=rank_of, reverse=True)
    for stage in order:
        other = swap(value, stage)
        lower = bit_of(stage) == 0
        place = sum(rank_of(s) > rank_of(stage) for s in held)
        value = jnp.stack(
            [jnp.where(lower, value, other), jnp.where(lower, other, value)], place
        )
        held.insert(place, stage)
    return value


def reduce_stage(value, stage, axis):
    mine = bit_of(stage)
    away = lax.dynamic_index_in_dim(value, 1 - mine, axis, keepdims=False).astype(bf16)
    kept = lax.dynamic_index_in_dim(value, mine, axis, keepdims=False)
    return kept, swap(away, stage)


def scatter_sum(value, order):
    bits = lax.axis_size("dp").bit_length() - 1
    rows, columns = value.shape[1], value.shape[3]
    value = value.reshape((2,) * bits + (rows, 2, columns))
    held = list(range(bits - 1, -1, -1)) + ["rows", "tp"]
    for stage in order:
        axis = held.index(stage)
        kept, arrived = reduce_stage(value, stage, axis)
        value = kept + arrived.astype(f32)
        held.pop(axis)
    return value


def sum_everywhere(value):
    bits = lax.axis_size("dp").bit_length() - 1
    for stage in [*range(bits), "tp"]:
        value = value + swap(value, stage)
    return value


def attend_kernel(height, q_ref, k_ref, v_ref, o_ref, lse_ref):
    first = lax.broadcasted_iota(jnp.int32, (1, PAIR), 1) < HEAD

    def step(index, carry):
        rows = pl.ds(pl.multiple_of(index * height, height), height)
        queries = q_ref[rows, :] * jnp.asarray(HEAD**-0.5, bf16)
        outs, totals = [], []
        for own in (first, ~first):
            scores = dot(jnp.where(own, queries, jnp.zeros_like(queries)), k_ref[...], NT)
            highest = jnp.max(scores, -1, keepdims=True)
            weights = jnp.exp(scores - highest)
            total = jnp.sum(weights, -1, keepdims=True)
            outs.append(dot(weights.astype(bf16), v_ref[...]) * (1.0 / total))
            totals.append(highest + jnp.log(total))
        o_ref[rows, :] = jnp.where(first, outs[0], outs[1])
        lse_ref[rows, :] = jnp.where(first, totals[0], totals[1])
        return carry

    lax.fori_loop(0, q_ref.shape[0] // height, step, 0)


def attend(queries, key_rows, value_rows, pair, height):
    count, full = queries.shape[0], key_rows.shape[0]
    narrow = pl.BlockSpec((count, PAIR), lambda step: (0, pair))
    wide = pl.BlockSpec((full, PAIR), lambda step: (0, pair))
    result = pl.BlockSpec((count, PAIR), lambda step: (0, 0))
    return pl.pallas_call(
        functools.partial(attend_kernel, height),
        grid=(1,),
        in_specs=[narrow, wide, wide],
        out_specs=[result, result],
        out_shape=[jax.ShapeDtypeStruct((count, PAIR), f32)] * 2,
        cost_estimate=pl.CostEstimate(
            flops=16 * count * full * PAIR, transcendentals=2 * count * full, bytes_accessed=4 * full * PAIR
        ),
        name="attend",
    )(queries, key_rows, value_rows)


def attend_back_kernel(
    height, q_ref, k_ref, v_ref, g_ref, o_ref, lse_ref, dq_ref, dk_ref, dv_ref, dk_sum, dv_sum
):
    first = lax.broadcasted_iota(jnp.int32, (1, PAIR), 1) < HEAD
    dk_sum[...] = jnp.zeros_like(dk_sum)
    dv_sum[...] = jnp.zeros_like(dv_sum)

    def step(index, carry):
        rows = pl.ds(pl.multiple_of(index * height, height), height)
        queries = q_ref[rows, :] * jnp.asarray(HEAD**-0.5, bf16)
        grads = g_ref[rows, :]
        products = grads.astype(f32) * o_ref[rows, :]
        query_grads = []
        for head, own in enumerate((first, ~first)):
            head_queries = jnp.where(own, queries, jnp.zeros_like(queries))
            head_grads = jnp.where(own, grads, jnp.zeros_like(grads))
            diagonal = jnp.sum(jnp.where(own, products, 0.0), -1, keepdims=True)
            log_total = lse_ref[rows, head * HEAD : head * HEAD + 1]
            weights = jnp.exp(dot(head_queries, k_ref[...], NT) - log_total)
            weight_grads = dot(head_grads, v_ref[...], NT)
            score_grads = (weights * (weight_grads - diagonal)).astype(bf16)
            dv_sum[...] += dot(weights.astype(bf16), head_grads, TN)
            dk_sum[...] += dot(score_grads, head_queries, TN)
            query_grads.append(dot(score_grads, k_ref[...]))
        dq_ref[rows, :] = (jnp.where(first, *query_grads) * HEAD**-0.5).astype(bf16)
        return carry

    lax.fori_loop(0, q_ref.shape[0] // height, step, 0)
    dk_ref[...] = dk_sum[...].astype(bf16)
    dv_ref[...] = dv_sum[...].astype(bf16)


def attend_back(queries, key_rows, value_rows, grads, mixed, log_total, pair, height):
    count, full = queries.shape[0], key_rows.shape[0]
    narrow = pl.BlockSpec((count, PAIR), lambda step: (0, pair))
    wide = pl.BlockSpec((full, PAIR), lambda step: (0, pair))
    alone = pl.BlockSpec((count, PAIR), lambda step: (0, 0))
    alone_wide = pl.BlockSpec((full, PAIR), lambda step: (0, 0))
    return pl.pallas_call(
        functools.partial(attend_back_kernel, height),
        grid=(1,),
        in_specs=[narrow, wide, wide, narrow, alone, alone],
        out_specs=[alone, alone_wide, alone_wide],
        out_shape=[
            jax.ShapeDtypeStruct((count, PAIR), bf16),
            jax.ShapeDtypeStruct((full, PAIR), bf16),
            jax.ShapeDtypeStruct((full, PAIR), bf16),
        ],
        scratch_shapes=[pltpu.VMEM((full, PAIR), f32)] * 2,
        cost_estimate=pl.CostEstimate(
            flops=40 * count * full * PAIR, transcendentals=2 * count * full, bytes_accessed=6 * full * PAIR
        ),
        name="attend_back",
    )(queries, key_rows, value_rows, grads, mixed, log_total)


def split(value):
    high = value.astype(bf16)
    return high, (value - high.astype(f32)).astype(bf16)


def triple(left, right, dims=NN):
    left_high, left_low = split(left)
    right_high, right_low = split(right)
    return dot(left_high, right_high, dims) + (
        dot(left_high, right_low, dims) + dot(left_low, right_high, dims)
    )


def orthogonal_kernel(x_ref, out_ref, gram_ref, power_ref):
    size = x_ref.shape[0]
    eye = lax.broadcasted_iota(jnp.int32, (size, size), 0) == lax.broadcasted_iota(
        jnp.int32, (size, size), 1
    )
    whole = x_ref[...]
    gram = dot(whole, whole, NT) if whole.dtype == bf16 else triple(whole, whole, NT)
    diagonal = jnp.where(eye, gram, 0.0)
    total = jnp.sum(jnp.sum(diagonal, 0, keepdims=True), 1, keepdims=True)
    inverse = 1.0 / (jnp.sqrt(total) + frob_eps)
    gram_ref[...] = gram * (inverse * inverse)
    power_ref[...] = jnp.where(eye, inverse, 0.0)

    def poly(gram):
        return (
            jnp.where(eye, coef_first, 0.0) + coef_second * gram + coef_third * triple(gram, gram)
        )

    def step(index, carry):
        gram = gram_ref[...]
        factor = poly(gram)
        power_ref[...] = triple(factor, power_ref[...])
        gram_ref[...] = triple(triple(gram, factor), factor)
        return carry

    lax.fori_loop(0, NS_STEPS - 1, step, 0)
    out_ref[...] = triple(poly(gram_ref[...]), power_ref[...])


def orthogonal_factor(matrix):
    size = matrix.shape[0]
    return pl.pallas_call(
        orthogonal_kernel,
        out_shape=jax.ShapeDtypeStruct((size, size), f32),
        scratch_shapes=[pltpu.VMEM((size, size), f32)] * 2,
        cost_estimate=pl.CostEstimate(
            flops=120 * size**3, transcendentals=0, bytes_accessed=4 * size * size
        ),
        name="orthogonal",
    )(matrix)


def layer_norm(inputs, gain_row, shift_row):
    average = jnp.mean(inputs, -1, keepdims=True)
    centred = inputs - average
    spread = jnp.mean(centred * centred, -1, keepdims=True)
    inverse = lax.rsqrt(spread + norm_eps)
    normed = centred * inverse
    return (normed * gain_row + shift_row, normed, inverse)


def norm_back(grad_out, normed, inverse, gain_row):
    scaled = grad_out * gain_row
    first_mean = jnp.mean(scaled, -1, keepdims=True)
    second_mean = jnp.mean(scaled * normed, -1, keepdims=True)
    return inverse * (scaled - first_mean - normed * second_mean)


def adam_step(vector, gradient, moment, square):
    moment_next = decay_first * moment + (1.0 - decay_first) * gradient
    square_next = decay_second * square + (1.0 - decay_second) * gradient * gradient
    moment_hat = moment_next / (1.0 - decay_first**STEP)
    square_hat = square_next / (1.0 - decay_second**STEP)
    return (
        vector - adam_rate * moment_hat / (jnp.sqrt(square_hat) + 1e-08),
        moment_next,
        square_next,
    )


def per_device(
    tokens,
    cotangent,
    query_weight,
    key_weight,
    value_weight,
    output_weight,
    up_weight,
    down_weight,
    query_momentum,
    key_momentum,
    value_momentum,
    output_momentum,
    up_momentum,
    down_momentum,
    norm_gains,
    block_biases,
    mixer_biases,
    hidden_bias,
    gains_first,
    gains_second,
    biases_first,
    biases_second,
    mixer_first,
    mixer_second,
    hidden_first,
    hidden_second,
):
    clip_count, half_len, width = tokens.shape
    assert clip_count == 1
    count = lax.axis_size("dp")
    bits = count.bit_length() - 1
    dp_index = lax.axis_index("dp")
    tp_index = lax.axis_index("tp")
    rows_here, part = query_weight.shape
    hidden_part = up_weight.shape[1]
    height = math.gcd(half_len, 112)
    far_first = [*range(bits - 1, 0, -1), "tp", 0]

    own_tokens = tokens.reshape(half_len, width)
    other_tokens = swap(own_tokens, "tp")
    small = jnp.concatenate([mixer_biases.reshape(-1), hidden_bias]).reshape(1, -1)
    both_small = gather_blocks(small, ["tp"]).reshape(2, -1)
    query_bias = both_small[:, :part].reshape(1, -1)
    value_bias = both_small[:, part : 2 * part].reshape(1, -1)
    up_bias = both_small[:, 2 * part :].reshape(1, -1)

    mixer_shard = jnp.concatenate(
        [query_weight, key_weight, value_weight, output_weight.T], 1
    ).astype(bf16)
    mixer_all = gather_blocks(mixer_shard, far_first).reshape(2, width, 4, part)
    mixer_all = mixer_all.transpose(2, 1, 0, 3).reshape(4, width, 2 * part)
    query_full, key_full, value_full, output_full = (mixer_all[j] for j in range(4))
    hidden_shard = jnp.concatenate([up_weight, down_weight.T], 1).astype(bf16)
    hidden_all = gather_blocks(hidden_shard, far_first).reshape(2, width, 2, hidden_part)
    hidden_all = hidden_all.transpose(2, 1, 0, 3).reshape(2, width, 2 * hidden_part)
    up_full, down_full = hidden_all[0], hidden_all[1]

    own_rows = own_tokens.astype(f32)
    normed_one, unit_one, inverse_one = layer_norm(own_rows, norm_gains[0], block_biases[0])
    normed_other, _, _ = layer_norm(other_tokens.astype(f32), norm_gains[0], block_biases[0])
    flat_one = normed_one.astype(bf16)
    clip_one = jnp.concatenate([flat_one, normed_other.astype(bf16)], 0)
    queries = (dot(flat_one, query_full) + query_bias).astype(bf16)
    key_rows = dot(clip_one, key_full).astype(bf16)
    value_rows = (dot(clip_one, value_full) + value_bias).astype(bf16)
    attended = [attend(queries, key_rows, value_rows, pair, height) for pair in range(HEADS // 2)]
    mixed_low = jnp.concatenate([mixed for mixed, _ in attended], 1).astype(bf16)
    residual = own_rows + dot(mixed_low, output_full, NT) + block_biases[1]
    normed_two, unit_two, inverse_two = layer_norm(residual, norm_gains[1], block_biases[2])
    flat_two = normed_two.astype(bf16)
    hidden_pre = dot(flat_two, up_full) + up_bias
    normal_cdf = 0.5 * (1.0 + lax.erf(hidden_pre * (1.0 / math.sqrt(2.0))))
    hidden_low = (hidden_pre * normal_cdf).astype(bf16)
    block_out = residual + dot(hidden_low, down_full, NT) + block_biases[3]

    cot_rows = cotangent.reshape(half_len, width)
    cot_low = cot_rows.astype(bf16)
    down_part = dot(cot_low, hidden_low, TN)
    slope = normal_cdf + hidden_pre * jnp.exp(-0.5 * hidden_pre * hidden_pre) * (
        1.0 / math.sqrt(2.0 * math.pi)
    )
    hidden_cot = (dot(cot_low, down_full) * slope).astype(bf16)
    hidden_local = jnp.sum(hidden_cot.astype(f32), 0)
    up_part = dot(flat_two, hidden_cot, TN)
    norm_cot_two = dot(hidden_cot, up_full, NT)
    residual_cot = cot_rows + norm_back(norm_cot_two, unit_two, inverse_two, norm_gains[1])
    residual_low = residual_cot.astype(bf16)
    output_part = dot(residual_low, mixed_low, TN)
    mixed_cot = dot(residual_low, output_full).astype(bf16)

    near_first = [0, "tp", *range(1, bits)]

    def blocks(partial_sum, size):
        return partial_sum.reshape(count, rows_here, 2, size)

    hidden_grads = scatter_sum(
        jnp.concatenate(
            [
                blocks(up_part, hidden_part),
                blocks(down_part, hidden_part),
                blocks(output_part, part),
            ],
            3,
        ),
        near_first,
    )
    up_grad = hidden_grads[:, :hidden_part]
    down_grad = hidden_grads[:, hidden_part : 2 * hidden_part]
    output_grad = hidden_grads[:, 2 * hidden_part :]

    backs = [
        attend_back(
            queries, key_rows, value_rows, mixed_cot, attended[pair][0], attended[pair][1], pair, height
        )
        for pair in range(HEADS // 2)
    ]
    query_cot = jnp.concatenate([back[0] for back in backs], 1)
    key_cot = jnp.concatenate([back[1] for back in backs], 1)
    value_cot = jnp.concatenate([back[2] for back in backs], 1)
    attention_grads = scatter_sum(
        jnp.concatenate(
            [
                blocks(dot(flat_one, query_cot, TN), part),
                blocks(dot(clip_one, key_cot, TN), part),
                blocks(dot(clip_one, value_cot, TN), part),
            ],
            3,
        ),
        near_first,
    )
    query_grad = attention_grads[:, :part]
    key_grad = attention_grads[:, part : 2 * part]
    value_grad = attention_grads[:, 2 * part :]

    back_both = dot(key_cot, key_full, NT) + dot(value_cot, value_full, NT)
    back_sent = swap(back_both[half_len:].astype(bf16), "tp")
    norm_cot_one = dot(query_cot, query_full, NT) + back_both[:half_len] + back_sent.astype(f32)
    input_grad = residual_cot + norm_back(norm_cot_one, unit_one, inverse_one, norm_gains[0])

    vector_sums = [
        jnp.sum(norm_cot_one * unit_one, 0),
        jnp.sum(norm_cot_two * unit_two, 0),
        jnp.sum(norm_cot_one, 0),
        jnp.sum(residual_cot, 0),
        jnp.sum(norm_cot_two, 0),
        jnp.sum(cot_rows, 0),
        jnp.sum(query_cot.astype(f32), 0),
        jnp.sum(value_cot.astype(f32), 0),
        hidden_local,
    ]
    summed = sum_everywhere(jnp.concatenate(vector_sums).reshape(-1, 128)).reshape(-1)
    gains_grad = summed[: 2 * width].reshape(2, width)
    biases_grad = summed[2 * width : 6 * width].reshape(4, width)
    mixer_whole = summed[6 * width : 8 * width].reshape(2, width)
    mixer_grad = lax.dynamic_slice_in_dim(mixer_whole, tp_index * part, part, 1)
    hidden_grad = lax.dynamic_slice_in_dim(
        summed[8 * width :], tp_index * hidden_part, hidden_part, 0
    )

    query_velocity = 0.5 * query_momentum + query_grad
    key_velocity = 0.5 * key_momentum + key_grad
    value_velocity = 0.5 * value_momentum + value_grad
    output_velocity = 0.5 * output_momentum.T + output_grad
    up_velocity = 0.5 * up_momentum + up_grad
    down_velocity = 0.5 * down_momentum.T + down_grad

    core, side = bit_of(0) == 0, bit_of(1) == 0

    def rows_for(matrix, mask):
        start = (dp_index ^ mask) * rows_here
        return lax.dynamic_slice_in_dim(matrix, start, rows_here, 0)

    kept = jnp.where(core, up_velocity, down_velocity).astype(bf16)
    sent = jnp.where(core, down_velocity, up_velocity).astype(bf16)
    arrived = swap(sent, 0)
    pair_rows = jnp.stack([jnp.where(core, kept, arrived), jnp.where(core, arrived, kept)], 0)
    own_half = gather_blocks(pair_rows, [*range(bits - 1, 0, -1)], (0,)).reshape(width, hidden_part)
    other_half = swap(own_half, "tp")
    factor = orthogonal_factor(jnp.concatenate([own_half, other_half], 1))
    mine, theirs = (
        jnp.dot(rows_for(factor, mask), own_half.astype(f32), precision=exact) for mask in (0, 1)
    )
    theirs = swap(theirs, 0)
    up_turn = jnp.where(core, mine, theirs)
    down_turn = jnp.where(core, theirs, mine)

    stacked = jnp.stack([query_velocity, key_velocity, value_velocity, output_velocity])
    stacked = stacked.reshape(2, 2, rows_here, part)
    kept = jnp.where(core, stacked[:, 0], stacked[:, 1])
    arrived = swap(jnp.where(core, stacked[:, 1], stacked[:, 0]), 0)
    pairs = jnp.stack([jnp.where(core, kept, arrived), jnp.where(core, arrived, kept)], 1)
    kept = jnp.where(side, pairs[0], pairs[1])
    arrived = swap(jnp.where(side, pairs[1], pairs[0]), 1)
    quads = jnp.stack([jnp.where(side, kept, arrived), jnp.where(side, arrived, kept)], 0)
    own_half = gather_blocks(quads, [*range(bits - 1, 1, -1)], (1, 0)).reshape(width, part)
    other_half = swap(own_half, "tp")
    factor = orthogonal_factor(jnp.concatenate([own_half, other_half], 1))
    four_rows = jnp.concatenate([rows_for(factor, mask) for mask in (0, 1, 2, 3)], 0)
    turned = jnp.dot(four_rows, own_half, precision=exact).reshape(2, 2, rows_here, part)
    arrived = swap(turned[:, 1], 0)
    kept = turned[:, 0]
    pairs = jnp.stack([jnp.where(core, kept, arrived), jnp.where(core, arrived, kept)], 1)
    arrived = swap(pairs[1], 1)
    query_turn, value_turn = jnp.where(side, pairs[0], arrived)[0], jnp.where(side, arrived, pairs[0])[0]
    key_turn, output_turn = jnp.where(side, pairs[0], arrived)[1], jnp.where(side, arrived, pairs[0])[1]

    directions = [query_turn, key_turn, value_turn, output_turn.T, up_turn, down_turn.T]
    factors_list = [1.0, 1.0, 1.0, 1.0, max(1.0, FF / D) ** 0.5, max(1.0, D / FF) ** 0.5]
    masters = [query_weight, key_weight, value_weight, output_weight, up_weight, down_weight]
    new_masters = [
        master - muon_rate * factor * direction
        for master, factor, direction in zip(masters, factors_list, directions)
    ]
    copies = [master.astype(bf16) for master in new_masters]
    gains_next, gains_moment, gains_square = adam_step(
        norm_gains, gains_grad, gains_first, gains_second
    )
    biases_next, biases_moment, biases_square = adam_step(
        block_biases, biases_grad, biases_first, biases_second
    )
    mixer_next, mixer_moment, mixer_square = adam_step(
        mixer_biases, mixer_grad, mixer_first, mixer_second
    )
    hidden_next, hidden_moment, hidden_square = adam_step(
        hidden_bias, hidden_grad, hidden_first, hidden_second
    )
    return (
        block_out.reshape(tokens.shape),
        input_grad.reshape(tokens.shape),
        query_grad,
        key_grad,
        value_grad,
        output_grad.T,
        up_grad,
        down_grad.T,
        query_velocity,
        key_velocity,
        value_velocity,
        output_velocity.T,
        up_velocity,
        down_velocity.T,
        *new_masters,
        *copies,
        gains_grad,
        biases_grad,
        mixer_grad,
        hidden_grad,
        gains_next,
        biases_next,
        mixer_next,
        hidden_next,
        gains_moment,
        biases_moment,
        mixer_moment,
        hidden_moment,
        gains_square,
        biases_square,
        mixer_square,
        hidden_square,
    )


def solution(mesh):
    placed = (
        P("dp", "tp", None),
        P("dp", "tp", None),
        P("dp", "tp"),
        P("dp", "tp"),
        P("dp", "tp"),
        P("tp", "dp"),
        P("dp", "tp"),
        P("tp", "dp"),
        P("dp", "tp"),
        P("dp", "tp"),
        P("dp", "tp"),
        P("tp", "dp"),
        P("dp", "tp"),
        P("tp", "dp"),
        P(),
        P(),
        P(None, "tp"),
        P("tp"),
        P(),
        P(),
        P(),
        P(),
        P(None, "tp"),
        P(None, "tp"),
        P("tp"),
        P("tp"),
    )
    return jax.shard_map(
        per_device,
        mesh=mesh,
        in_specs=placed,
        out_specs=(
            P("dp", "tp", None),
            P("dp", "tp", None),
            P("dp", "tp"),
            P("dp", "tp"),
            P("dp", "tp"),
            P("tp", "dp"),
            P("dp", "tp"),
            P("tp", "dp"),
            P("dp", "tp"),
            P("dp", "tp"),
            P("dp", "tp"),
            P("tp", "dp"),
            P("dp", "tp"),
            P("tp", "dp"),
            P("dp", "tp"),
            P("dp", "tp"),
            P("dp", "tp"),
            P("tp", "dp"),
            P("dp", "tp"),
            P("tp", "dp"),
            P("dp", "tp"),
            P("dp", "tp"),
            P("dp", "tp"),
            P("tp", "dp"),
            P("dp", "tp"),
            P("tp", "dp"),
            P(),
            P(),
            P(None, "tp"),
            P("tp"),
            P(),
            P(),
            P(None, "tp"),
            P("tp"),
            P(),
            P(),
            P(None, "tp"),
            P("tp"),
            P(),
            P(),
            P(None, "tp"),
            P("tp"),
        ),
        check_vma=False,
    )
```
